32 devices in a mesh: sensor: 16 (over z, x, core), batch: 2 (over y).
Axes of the slice: x: 2, y: 2, z: 4, core: 2. Of those that a mesh axis runs over, the one named last changes fastest.
Arguments:
- pixels: bfloat16 [64, 1024, 832], P(('sensor', 'batch')), may hold values from -6 to 6
- visible: int32 [64, 256], P(('sensor', 'batch')), may hold values from 0 to 1023, as said below
- chip_size: int32 [64], P(('sensor', 'batch')), may hold values from 256 to 1024, as said below
- sensor_id: int32 [64], P(('sensor', 'batch')), may hold values from 0 to 3, as said below
- band_count: int32 [4], replicated, may hold values from 3 to 13
- wavelengths: float32 [4, 13], replicated, may hold values from 0.4 to 2.4
- time_place: float32 [64, 8], P(('sensor', 'batch')), may hold values from -1 to 1
- cls_token: float32 [768], replicated, may hold values from -5 to 5
- w_meta: bfloat16 [8, 768], replicated, may hold values from -2 to 2
- w_wave1: bfloat16 [128, 128], replicated, may hold values from -0.5 to 0.5
- wave1_bias: float32 [128], replicated, may hold values from -3 to 3
- w_wave2: bfloat16 [49152, 128], P(('sensor', 'batch')), may hold values from -0.02734375 to 0.02734375
- patch_bias: float32 [768], replicated, may hold values from -2 to 2
- ln1_gain: float32 [768], replicated, may hold values from 0.5 to 1.5
- ln1_bias: float32 [768], replicated, may hold values from -2 to 2
- w_qkv: bfloat16 [768, 2304], P(('sensor', 'batch')), may hold values from -0.21875 to 0.21875
- w_out: bfloat16 [768, 768], P(('sensor', 'batch')), may hold values from -1.75 to 1.75
- out_bias: float32 [768], replicated, may hold values from -2 to 2
- ln2_gain: float32 [768], replicated, may hold values from 0.5 to 1.5
- ln2_bias: float32 [768], replicated, may hold values from -2 to 2
- w_fc1: bfloat16 [768, 3072], P(('sensor', 'batch')), may hold values from -0.21875 to 0.21875
- fc1_bias: float32 [3072], replicated, may hold values from -3 to 3
- w_fc2: bfloat16 [3072, 768], P(('sensor', 'batch')), may hold values from -0.109375 to 0.109375
- fc2_bias: float32 [768], replicated, may hold values from -2 to 2
- cotangent: bfloat16 [64, 258, 768], P(('sensor', 'batch')), may hold values from -6 to 6
Outputs:
- mixed: bfloat16 [64, 258, 768], P(('sensor', 'batch'))
- grad_pixels: float32 [64, 1024, 832], P(('sensor', 'batch'))
- grad_time_place: float32 [64, 8], P(('sensor', 'batch'))
- grad_cls: float32 [768], replicated
- grad_w_meta: float32 [8, 768], replicated
- grad_w_wave1: float32 [128, 128], replicated
- grad_wave1_bias: float32 [128], replicated
- grad_w_wave2: float32 [49152, 128], P(('sensor', 'batch'))
- grad_patch_bias: float32 [768], replicated
- grad_ln1_gain: float32 [768], replicated
- grad_ln1_bias: float32 [768], replicated
- grad_w_qkv: float32 [768, 2304], P(('sensor', 'batch'))
- grad_w_out: float32 [768, 768], P(('sensor', 'batch'))
- grad_out_bias: float32 [768], replicated
- grad_ln2_gain: float32 [768], replicated
- grad_ln2_bias: float32 [768], replicated
- grad_w_fc1: float32 [768, 3072], P(('sensor', 'batch'))
- grad_fc1_bias: float32 [3072], replicated
- grad_w_fc2: float32 [3072, 768], P(('sensor', 'batch'))
- grad_fc2_bias: float32 [768], replicated
The draws below stay inside these ranges and needn't reach their ends.
Inputs may be any that keep to these rules, and one draw needn't show every extreme that they name: `chip_size`: each is 1024 or 256. `visible`: each chip's entries are distinct patches below its chip_size; for a chip of 256 patches only the first 64 entries are read. `sensor_id`: each sensor has exactly 16 chips, anywhere among the chips.
All inputs are finite; a program needn't handle non-finite values.
Results may differ from the reference program's by a relative error of at most 0.02.
Values may be sent and summed in bfloat16 or wider, within the bound.
No kernel may reach another device: no remote copies, remote signals or barrier semaphores. Data moves between devices by JAX's collectives and lax.ppermute only.
A program may use at most 256 MiB of HBM per device.

```python
import math
import jax
import jax.numpy as jnp
from jax import lax

D = 768
HEADS = 12
HEAD_DIM = 64
FF = 3072
HYPER = 128
BANDS = 13
META = 8
SIDE = 32
SENSORS = 4
CHIPS = 64
PIXW = 832
KCOLS = 49152
MAXP = 1024
VIS_MAX = 256
LEN = 258


def size_pick(key):
    coins = jax.random.randint(jax.random.fold_in(key, 11), (CHIPS,), 0, 2)
    spots = jax.random.permutation(jax.random.fold_in(key, 12), CHIPS)
    position = jnp.arange(CHIPS)
    larger = (coins == 1) | (position == spots[0])
    larger = larger & (position != spots[1])
    return jnp.where(larger, MAXP, MAXP // 4).astype(jnp.int32)


def draw_chip_size(key, part):
    return size_pick(key)


def draw_visible(key, part):
    chip_sizes = size_pick(key)
    subkeys = jax.random.split(jax.random.fold_in(key, 13), CHIPS)
    larger = jax.vmap(lambda subkey: jax.random.permutation(subkey, MAXP)[:VIS_MAX])(subkeys)
    smaller = jax.vmap(lambda subkey: jax.random.permutation(jax.random.fold_in(subkey, 1), MAXP // 4))(subkeys)
    return jnp.where(chip_sizes[:, None] == MAXP, larger, smaller).astype(jnp.int32)


def draw_sensor_id(key, part):
    order = jax.random.permutation(jax.random.fold_in(key, 31), CHIPS).astype(jnp.int32)
    return (order % SENSORS).astype(jnp.int32)


def draw_band_count(key, part):
    lowest = max(1, BANDS - 10)
    counts = jax.random.randint(jax.random.fold_in(key, 21), (SENSORS,), lowest, BANDS + 1)
    chosen = jax.random.randint(jax.random.fold_in(key, 22), (), 0, SENSORS)
    lesser = jax.random.randint(jax.random.fold_in(key, 23), (), lowest, BANDS)
    position = jnp.arange(SENSORS)
    following = (chosen + 1) % SENSORS
    counts = jnp.where(position == following, lesser, counts)
    return jnp.where(position == chosen, BANDS, counts).astype(jnp.int32)


def block_scale(rng, extent, pieces, low, top_value):
    def one(dim, shards_of):
        heights = jax.random.uniform(jax.random.fold_in(jax.random.fold_in(rng, 6), dim), (shards_of,), jnp.float32, low / len(pieces), top_value / len(pieces))
        return jnp.repeat(jnp.exp(heights), extent[dim] // shards_of).reshape((-1,) + (1,) * (len(extent) - dim - 1))

    loudness = one(*pieces[0])
    for cut in pieces[1:]:
        loudness = loudness * one(*cut)
    return loudness


def noise(own_key, shape, deviation, reach, cuts=(), kind=jnp.bfloat16):
    drawn = jax.random.normal(own_key, shape, jnp.float32) * deviation
    if len(cuts) > 0:
        drawn = block_scale(own_key, shape, cuts, -0.22, 0.18) * drawn
    return jnp.clip(drawn, min=-reach, max=reach).astype(kind)


def setup_inputs(seed: int = 0) -> dict:
    seeds = jax.random.split(jax.random.key(seed), 26)
    return {
        "pixels": noise(seeds[0], (CHIPS, MAXP, PIXW), 1.0, 6.0, ((0, 32),)),
        "visible": draw_visible(jax.random.fold_in(seeds[25], 71), 0),
        "chip_size": draw_chip_size(jax.random.fold_in(seeds[25], 71), 0),
        "sensor_id": draw_sensor_id(jax.random.fold_in(seeds[25], 71), 0),
        "band_count": draw_band_count(jax.random.fold_in(seeds[25], 71), 0),
        "wavelengths": jnp.clip(jax.random.uniform(seeds[5], (SENSORS, BANDS), jnp.float32, 0.4, 2.4), 0.4, 2.4),
        "time_place": jnp.clip(jax.random.uniform(seeds[6], (CHIPS, META), jnp.float32, -1.0, 1.0) * block_scale(seeds[6], (CHIPS, META), ((0, 32),), -0.4, 0.0), -1.0, 1.0),
        "cls_token": noise(seeds[7], (D,), 1.0, 5.0, (), jnp.float32),
        "w_meta": noise(seeds[8], (META, D), META ** -0.5, 2.0),
        "w_wave1": noise(seeds[9], (HYPER, HYPER), HYPER ** -0.5, 0.5),
        "wave1_bias": noise(seeds[10], (HYPER,), 0.5, 3.0, (), jnp.float32),
        "w_wave2": noise(seeds[11], (KCOLS, HYPER), (HYPER * PIXW // 2) ** -0.5, 0.02734375, ((0, 32),)),
        "patch_bias": noise(seeds[12], (D,), 0.3, 2.0, (), jnp.float32),
        "ln1_gain": jnp.clip(1.0 + 0.1 * jax.random.normal(seeds[13], (D,), jnp.float32), 0.5, 1.5),
        "ln1_bias": noise(seeds[14], (D,), 0.3, 2.0, (), jnp.float32),
        "w_qkv": noise(seeds[15], (D, 3 * D), D ** -0.5, 0.21875, ((0, 32),)),
        "w_out": noise(seeds[16], (D, D), (max(1, D // 64)) ** -0.5, 1.75, ((0, 32),)),
        "out_bias": noise(seeds[17], (D,), 0.3, 2.0, (), jnp.float32),
        "ln2_gain": jnp.clip(1.0 + 0.1 * jax.random.normal(seeds[18], (D,), jnp.float32), 0.5, 1.5),
        "ln2_bias": noise(seeds[19], (D,), 0.3, 2.0, (), jnp.float32),
        "w_fc1": noise(seeds[20], (D, FF), D ** -0.5, 0.21875, ((0, 32),)),
        "fc1_bias": noise(seeds[21], (FF,), 0.5, 3.0, (), jnp.float32),
        "w_fc2": noise(seeds[22], (FF, D), FF ** -0.5, 0.109375, ((0, 32),)),
        "fc2_bias": noise(seeds[23], (D,), 0.3, 2.0, (), jnp.float32),
        "cotangent": noise(seeds[24], (CHIPS, LEN, D), 1.0, 6.0, ((0, 32),)),
    }


@jax.custom_vjp
def low(v):
    return lax.optimization_barrier(v.astype(jnp.bfloat16)).astype(jnp.float32)

@jax.custom_vjp
def low_back(v):
    return v

def low_keep(v):
    return (low(v), None)

def low_pass(kept, grad):
    return (grad,)

def back_keep(v):
    return (v, None)

def back_low(kept, grad):
    return (low(grad),)
low.defvjp(low_keep, low_pass)
low_back.defvjp(back_keep, back_low)
PRECISE = lax.Precision.HIGHEST
EPSILON = 1e-05

def wave_code(wavelengths):
    halfwidth = HYPER // 2
    freqs = 10000.0 ** (-jnp.arange(halfwidth, dtype=jnp.float32) / halfwidth)
    angles = (wavelengths * 1000.0)[:, :, None] * freqs
    return jnp.concatenate([jnp.sin(angles), jnp.cos(angles)], axis=-1)

def place_code(visible, chip_size):
    side_len = jnp.where(chip_size == MAXP, SIDE, SIDE // 2).astype(jnp.int32)
    row_pos = (visible // side_len[:, None]).astype(jnp.float32)
    col_pos = (visible % side_len[:, None]).astype(jnp.float32)
    quarter = D // 4
    freqs = 10000.0 ** (-jnp.arange(quarter, dtype=jnp.float32) / quarter)
    row_ang = row_pos[..., None] * freqs
    col_ang = col_pos[..., None] * freqs
    return jnp.concatenate([jnp.sin(row_ang), jnp.cos(row_ang), jnp.sin(col_ang), jnp.cos(col_ang)], axis=-1)

def layer_norm(values, gain, offset):
    center = values - lax.optimization_barrier(jnp.mean(values, axis=-1, keepdims=True))
    spread = lax.optimization_barrier(jnp.mean(center * center, axis=-1, keepdims=True))
    return center * lax.rsqrt(spread + EPSILON) * gain + offset

def reference(pixels, visible, chip_size, sensor_id, band_count, wavelengths, time_place, cls_token, w_meta, w_wave1, wave1_bias, w_wave2, patch_bias, ln1_gain, ln1_bias, w_qkv, w_out, out_bias, ln2_gain, ln2_bias, w_fc1, fc1_bias, w_fc2, fc2_bias, cotangent):
    single = jnp.float32
    params = (pixels.astype(single), time_place, cls_token, w_meta.astype(single), w_wave1.astype(single), wave1_bias, w_wave2.astype(single), patch_bias, ln1_gain, ln1_bias, w_qkv.astype(single), w_out.astype(single), out_bias, ln2_gain, ln2_bias, w_fc1.astype(single), fc1_bias, w_fc2.astype(single), fc2_bias)
    code = wave_code(wavelengths).reshape(SENSORS * BANDS, HYPER)
    band_mask = (jnp.arange(BANDS)[None, :] < band_count[:, None]).astype(single).reshape(SENSORS * BANDS, 1)
    group = math.gcd(CHIPS, 16)
    blocks = CHIPS // group
    valid = (jnp.arange(LEN)[None, :] < (2 + chip_size // 4)[:, None]).astype(single)
    scale = HEAD_DIM ** (-0.5)

    def forward(pix, tplace, cls_vec, wmeta, wone, bone, wtwo, pbias, gain_one, bias_one, wqkv, wout, bout, gain_two, bias_two, wup, bup, wdown, bdown):
        pre_act = jnp.dot(code, wone, precision=PRECISE) + bone
        embed = jax.nn.gelu(pre_act, approximate=False) * band_mask
        kernel = low(jnp.dot(low(embed), wtwo.T, precision=PRECISE)).reshape(SENSORS, PIXW, D)

        def block(inputs):
            pix_b, vis_b, size_b, sid_b, tp_b, val_b = inputs
            patches = jnp.take_along_axis(pix_b, vis_b[:, :, None], axis=1)
            kern_b = kernel[sid_b]
            embedded = low_back(jnp.einsum('cvp,cpd->cvd', patches, kern_b, precision=PRECISE))
            tokens = embedded + place_code(vis_b, size_b) + pbias
            meta_tok = jnp.dot(tp_b, wmeta, precision=PRECISE)
            first = jnp.broadcast_to(cls_vec, (group, 1, D))
            start = jnp.concatenate([first, meta_tok[:, None, :], tokens], axis=1)
            normed = low(layer_norm(start, gain_one, bias_one))
            joined = jnp.einsum('cld,de->cle', normed, wqkv, precision=PRECISE)
            query = low(low_back(joined[..., :D])).reshape(group, LEN, HEADS, HEAD_DIM)
            keyed = low(low_back(joined[..., D:2 * D])).reshape(group, LEN, HEADS, HEAD_DIM)
            valued = low(low_back(joined[..., 2 * D:])).reshape(group, LEN, HEADS, HEAD_DIM)
            scores = low_back(jnp.einsum('cqhe,ckhe->chqk', query, keyed, precision=PRECISE) * scale)
            scores = jnp.where(val_b[:, None, None, :] > 0.5, scores, -1e+30)
            top_s = lax.optimization_barrier(jnp.max(scores, axis=-1, keepdims=True))
            expd = jnp.exp(scores - top_s)
            probs = expd / lax.optimization_barrier(jnp.sum(expd, axis=-1, keepdims=True))
            attn = jnp.einsum('chqk,ckhe->cqhe', low(probs), valued, precision=PRECISE).reshape(group, LEN, D)
            attn = low(low_back(attn))
            branch = low_back(jnp.einsum('cld,de->cle', attn, wout, precision=PRECISE) + bout)
            middle = start + branch
            normed_two = low(layer_norm(middle, gain_two, bias_two))
            pre_up = low_back(jnp.einsum('cld,df->clf', normed_two, wup, precision=PRECISE) + bup)
            hidden = low(jax.nn.gelu(pre_up, approximate=False))
            branch_two = low_back(jnp.einsum('clf,fd->cld', hidden, wdown, precision=PRECISE) + bdown)
            return (middle + branch_two) * val_b[:, :, None]
        stacked = (pix.reshape(blocks, group, MAXP, PIXW), visible.reshape(blocks, group, VIS_MAX), chip_size.reshape(blocks, group), sensor_id.reshape(blocks, group), tplace.reshape(blocks, group, META), valid.reshape(blocks, group, LEN))
        result = lax.map(jax.checkpoint(block), stacked)
        return result.reshape(CHIPS, LEN, D)
    output, pullback = jax.vjp(forward, *params)
    grads = pullback(cotangent.astype(single))
    return (output.astype(jnp.bfloat16), grads[0], grads[1], grads[2], grads[3], grads[4], grads[5], grads[6], grads[7], grads[8], grads[9], grads[10], grads[11], grads[12], grads[13], grads[14], grads[15], grads[16], grads[17], grads[18])
```

```python
import functools
import math

import jax
import jax.numpy as jnp
from jax import lax
from jax.experimental import pallas as pl
from jax.experimental.pallas import tpu as pltpu
from jax.sharding import PartitionSpec as P

D = 768
HEADS = 12
HYPER = 128
SIDE = 32
MAXP = 1024
AXES = ("sensor", "batch")

PRECISE = lax.Precision.HIGHEST
EPSILON = 1e-05
MASKED = -1e30
SINGLE = jnp.float32
HALF = jnp.bfloat16


def bit_groups(count):
    bits = count.bit_length() - 1
    high = list(range(3, bits))
    groups = [high[i : i + 2] for i in range(0, len(high), 2)]
    groups.append([b for b in (0, 2) if b < bits])
    if bits > 1:
        groups.append([1])
    return groups


def masks_of(group):
    masks = [0]
    for b in group:
        masks = masks + [m ^ (1 << b) for m in masks]
    return masks


def swap(values, mask, count):
    return lax.ppermute(values, AXES, [(i, i ^ mask) for i in range(count)])


def place_kernel(offsets, splits, index_ref, *refs):
    pieces, refs = refs[: len(offsets)], refs[len(offsets) :]
    outs, refs = refs[: 1 + max(s[0] for s in splits)], refs[1 + max(s[0] for s in splits) :]
    staged, in_sems, out_sems = refs
    me = index_ref[0]
    arrivals, departures = [], []
    first = 0
    for i, piece in enumerate(pieces):
        size = piece.shape[0]
        arrivals.append(
            pltpu.make_async_copy(piece, staged.at[pl.ds(first, size)], in_sems.at[i])
        )
        arrivals[-1].start()
        first += size
    first = 0
    for arrival, masks in zip(arrivals, offsets):
        arrival.wait()
        for t, mask in enumerate(masks):
            for which, slot, start, size in splits:
                target = outs[which].at[me ^ mask]
                departures.append(
                    pltpu.make_async_copy(
                        staged.at[first + t, :, pl.ds(start, size)],
                        target if slot is None else target.at[slot],
                        out_sems.at[len(departures)],
                    )
                )
                departures[-1].start()
        first += len(masks)
    for departure in departures:
        departure.wait()


def place(pieces, masks, splits, shapes, index, count):
    kind = pieces[0].dtype
    row = pieces[0].shape[1:]
    return pl.pallas_call(
        functools.partial(place_kernel, masks, splits),
        out_shape=[jax.ShapeDtypeStruct((count, *s), kind) for s in shapes],
        in_specs=[pl.BlockSpec(memory_space=pltpu.SMEM)]
        + [pl.BlockSpec(memory_space=pl.ANY)] * len(pieces),
        out_specs=[pl.BlockSpec(memory_space=pl.ANY)] * len(shapes),
        scratch_shapes=[
            pltpu.VMEM((count, *row), kind),
            pltpu.SemaphoreType.DMA((len(pieces),)),
            pltpu.SemaphoreType.DMA((count * len(splits),)),
        ],
        compiler_params=pltpu.CompilerParams(vmem_limit_bytes=32 * 2**20),
        cost_estimate=pl.CostEstimate(
            flops=0,
            bytes_accessed=4 * count * math.prod(row),
            transcendentals=0,
        ),
        name="place",
    )(index, *pieces)


def gather(shards, index, count):
    rows = min(s.shape[0] for s in shards)
    columns, splits, shapes = [], [], []
    start = 0
    for which, shard in enumerate(shards):
        parts = shard.shape[0] // rows
        shapes.append((parts, rows, shard.shape[1]) if parts > 1 else (rows, shard.shape[1]))
        for i in range(parts):
            columns.append(shard[i * rows : (i + 1) * rows])
            splits.append((which, i if parts > 1 else None, start, shard.shape[1]))
            start += shard.shape[1]
    groups = bit_groups(count)
    data, masks = jnp.concatenate(columns, axis=1)[None], [0]
    for group in groups[:-2]:
        ours = masks_of(group)
        data = jnp.concatenate(
            [data] + [swap(data, m, count) for m in ours[1:]], axis=0
        )
        masks = [m ^ q for m in ours for q in masks]
    pieces = [(masks, data)]
    for group in groups[-2:]:
        pieces = pieces + [
            ([m ^ q for q in held], swap(piece, m, count))
            for m in masks_of(group)[1:]
            for held, piece in pieces
        ]
    wholes = place(
        [p for _, p in pieces], [m for m, _ in pieces], splits, shapes, index, count
    )
    return [w.reshape(-1, w.shape[-1]) for w in wholes]


def chosen_half(values, bits, group, mask, index):
    starts, sizes, shape = [], [], []
    for b in bits:
        if b in group:
            starts.append(((index[0] ^ mask) >> b) & 1)
            sizes.append(1)
        else:
            starts.append(0)
            sizes.append(2)
            shape.append(2)
    tail = values.shape[len(bits) :]
    zeros = [0] * len(tail)
    return lax.dynamic_slice(values, starts + zeros, sizes + list(tail)).reshape(
        *shape, *tail
    )


def scatter(wholes, index, count):
    bits = list(range(count.bit_length() - 2, -1, -1))
    rows = min(w.shape[0] for w in wholes) // count
    kind = wholes[0].dtype
    views, columns, start = [], [], 0
    for whole in wholes:
        k = whole.shape[0] // count // rows
        view = whole.reshape([2] * len(bits) + [k, rows, whole.shape[1]])
        for i in range(k):
            columns.append((len(views), i, start, whole.shape[1]))
            start += whole.shape[1]
        views.append(view)
    received = []
    done = []

    def part(mask):
        pieces = []
        own = [chosen_half(v, bits, done, mask, index) for v in views]
        others = [chosen_half(v, left, done, mask, index) for v, left in received]
        for which, i, first, width in columns:
            piece = own[which][..., i, :, :]
            if others:
                piece = piece.astype(SINGLE)
                for other in others:
                    piece = piece + other[..., first : first + width].astype(SINGLE)
            pieces.append(piece)
        return pieces

    for group in reversed(bit_groups(count)):
        done = done + group
        arrived = []
        for m in masks_of(group)[1:]:
            sent = jnp.concatenate([p.astype(kind) for p in part(m)], axis=-1)
            arrived.append((swap(sent, m, count), [b for b in bits if b not in done]))
        received = received + arrived
    pieces = part(0)
    out = []
    for which in range(len(views)):
        mine = [p for p, c in zip(pieces, columns) if c[0] == which]
        out.append(jnp.concatenate(mine, axis=0) if len(mine) > 1 else mine[0])
    return out


def tree_sum(values):
    while len(values) > 1:
        values = [values[i] + values[i + 1] for i in range(0, len(values), 2)]
    return values[0]


def total_over(values, count):
    for group in reversed(bit_groups(count)):
        values = tree_sum(
            [values if m == 0 else swap(values, m, count) for m in masks_of(group)]
        )
    return values


def scores_of(keyed, query, lanes, key_ok):
    own = jnp.where(lanes, keyed, jnp.zeros_like(keyed))
    scores = lax.dot_general(
        own, query, (((1,), (1,)), ((), ())), preferred_element_type=SINGLE
    )
    scores = jnp.where(key_ok, scores, MASKED)
    expd = jnp.exp(scores - jnp.max(scores, axis=0, keepdims=True))
    return expd / jnp.sum(expd, axis=0, keepdims=True)


def over_rows(left, right):
    return lax.dot_general(
        left, right, (((0,), (0,)), ((), ())), preferred_element_type=SINGLE
    )


def attend_kernel(width, scale, count_ref, qkv_ref, out_ref):
    rows = qkv_ref.shape[1]
    head_dim = width // HEADS
    limit = count_ref[pl.program_id(0)]
    lane = lax.broadcasted_iota(jnp.int32, (rows, 128), 1) // head_dim
    key_ok = lax.broadcasted_iota(jnp.int32, (rows, rows), 0) < limit

    @pl.loop(0, width // 128)
    def _(pair):
        start = pl.multiple_of(pair * 128, 128)
        query = qkv_ref[0, :, pl.ds(start, 128)] * jnp.asarray(scale, HALF)
        keyed = qkv_ref[0, :, pl.ds(pl.multiple_of(width + start, 128), 128)]
        valued = qkv_ref[0, :, pl.ds(pl.multiple_of(2 * width + start, 128), 128)]
        result = jnp.zeros((rows, 128), SINGLE)
        for head in range(128 // head_dim):
            probs = scores_of(keyed, query, lane == head, key_ok)
            result = jnp.where(
                lane == head, over_rows(probs.astype(HALF), valued), result
            )
        out_ref[0, :, pl.ds(start, 128)] = result.astype(HALF)


def attend_back_kernel(width, scale, count_ref, qkv_ref, up_ref, out_ref):
    rows = qkv_ref.shape[1]
    head_dim = width // HEADS
    limit = count_ref[pl.program_id(0)]
    lane = lax.broadcasted_iota(jnp.int32, (rows, 128), 1) // head_dim
    key_ok = lax.broadcasted_iota(jnp.int32, (rows, rows), 0) < limit

    @pl.loop(0, width // 128)
    def _(pair):
        start = pl.multiple_of(pair * 128, 128)
        at_key = pl.multiple_of(width + start, 128)
        at_value = pl.multiple_of(2 * width + start, 128)
        query = qkv_ref[0, :, pl.ds(start, 128)] * jnp.asarray(scale, HALF)
        keyed = qkv_ref[0, :, pl.ds(at_key, 128)]
        valued = qkv_ref[0, :, pl.ds(at_value, 128)]
        upstream = up_ref[0, :, pl.ds(start, 128)]
        grad_q = jnp.zeros((rows, 128), SINGLE)
        grad_k = jnp.zeros((rows, 128), SINGLE)
        grad_v = jnp.zeros((rows, 128), SINGLE)
        for head in range(128 // head_dim):
            own = lane == head
            probs = scores_of(keyed, query, own, key_ok)
            grad_v = jnp.where(
                own,
                jnp.dot(probs.astype(HALF), upstream, preferred_element_type=SINGLE),
                grad_v,
            )
            grad_prob = lax.dot_general(
                jnp.where(own, valued, jnp.zeros_like(valued)),
                upstream,
                (((1,), (1,)), ((), ())),
                preferred_element_type=SINGLE,
            )
            inner = jnp.sum(probs * grad_prob, axis=0, keepdims=True)
            grad_score = (probs * (grad_prob - inner)).astype(HALF)
            grad_k = jnp.where(
                own, jnp.dot(grad_score, query, preferred_element_type=SINGLE), grad_k
            )
            grad_q = jnp.where(own, over_rows(grad_score, keyed), grad_q)
        out_ref[0, :, pl.ds(start, 128)] = (grad_q * scale).astype(HALF)
        out_ref[0, :, pl.ds(at_key, 128)] = grad_k.astype(HALF)
        out_ref[0, :, pl.ds(at_value, 128)] = grad_v.astype(HALF)


def attention_call(kernel, name, counts, arrays, out_width, flops):
    chips, rows = arrays[0].shape[:2]

    def spec(columns):
        return pl.BlockSpec((1, rows, columns), lambda c, counts: (c, 0, 0))

    return pl.pallas_call(
        kernel,
        out_shape=jax.ShapeDtypeStruct((chips, rows, out_width), HALF),
        grid_spec=pltpu.PrefetchScalarGridSpec(
            num_scalar_prefetch=1,
            grid=(chips,),
            in_specs=[spec(a.shape[2]) for a in arrays],
            out_specs=spec(out_width),
        ),
        compiler_params=pltpu.CompilerParams(vmem_limit_bytes=40 * 2**20),
        cost_estimate=pl.CostEstimate(
            flops=flops, bytes_accessed=10 * 2**20, transcendentals=2 * 2**20
        ),
        name=name,
    )(counts, *arrays)


def wave_code(wavelengths):
    halfwidth = HYPER // 2
    freqs = 10000.0 ** (-jnp.arange(halfwidth, dtype=SINGLE) / halfwidth)
    angles = (wavelengths * 1000.0)[:, :, None] * freqs
    return jnp.concatenate([jnp.sin(angles), jnp.cos(angles)], axis=-1)


def norm_forward(values, gain, offset):
    center = values - jnp.mean(values, axis=-1, keepdims=True)
    inv_std = lax.rsqrt(jnp.mean(center * center, axis=-1, keepdims=True) + EPSILON)
    normed = center * inv_std
    return (normed * gain + offset, normed, inv_std)


def norm_backward(upstream, normed, inv_std, gain):
    scaled = upstream * gain
    back = inv_std * (
        scaled
        - jnp.mean(scaled, axis=-1, keepdims=True)
        - normed * jnp.mean(scaled * normed, axis=-1, keepdims=True)
    )
    return (back, jnp.sum(upstream * normed, axis=0), jnp.sum(upstream, axis=0))


def gelu_parts(values):
    cumul = 0.5 * (1.0 + lax.erf(values * 0.5**0.5))
    density = jnp.exp(-0.5 * values * values) * (2.0 * math.pi) ** (-0.5)
    return (values * cumul, cumul + values * density)


def split_dot(form, exact, other):
    upper = exact.astype(HALF)
    lower = (exact - upper.astype(SINGLE)).astype(HALF)
    first_term = jnp.einsum(form, upper, other, preferred_element_type=SINGLE)
    return first_term + jnp.einsum(form, lower, other, preferred_element_type=SINGLE)


def local(
    count,
    pixels,
    visible,
    chip_size,
    sensor_id,
    band_count,
    wavelengths,
    time_place,
    cls_token,
    w_meta,
    w_wave1,
    wave1_bias,
    w_wave2,
    patch_bias,
    ln1_gain,
    ln1_bias,
    w_qkv,
    w_out,
    out_bias,
    ln2_gain,
    ln2_bias,
    w_fc1,
    fc1_bias,
    w_fc2,
    fc2_bias,
    cotangent,
):
    chips, patches_all, pix_width = pixels.shape
    sensors, bands = wavelengths.shape
    length, width = cotangent.shape[1:]
    seen = visible.shape[1]
    lead = length - seen
    rows = -(-length // 16) * 16
    rows_all = chips * rows
    spots = pix_width // bands
    scale = (width // HEADS) ** (-0.5)
    me = lax.axis_index(AXES).astype(jnp.int32).reshape(1)

    code = wave_code(wavelengths).reshape(sensors * bands, -1)
    band_mask = (
        (jnp.arange(bands)[None, :] < band_count[:, None]).astype(SINGLE).reshape(-1, 1)
    )
    pre_act = jnp.dot(code, w_wave1.astype(SINGLE), precision=PRECISE) + wave1_bias
    activ, activ_slope = gelu_parts(pre_act)
    embed_low = (activ * band_mask).astype(HALF)
    columns = w_wave2.shape[0]
    held = max(1, columns // width)
    per_row = columns // held
    pieces = width // per_row
    wave2_own = w_wave2.reshape(held, per_row, -1)
    kernel_own = (
        jnp.einsum("rh,pch->prc", embed_low, wave2_own, preferred_element_type=SINGLE)
        .astype(HALF)
        .reshape(held * sensors * bands, per_row)
    )
    generated = gather([kernel_own], me, count)[0]
    generated = (
        generated.reshape(spots // held, pieces, held * sensors * bands, per_row)
        if pieces > 1
        else generated
    )
    if pieces > 1:
        generated = generated.transpose(0, 2, 1, 3)
    generated = generated.reshape(spots * sensors * bands, width)

    proj_qkv, proj_out = gather([w_qkv, w_out], me, count)
    proj_down, proj_up = gather([w_fc2, w_fc1], me, count)

    spot_of = jnp.pad(visible, ((0, 0), (lead, rows - length)), constant_values=-1)
    token = jnp.arange(rows)
    is_patch = ((token >= lead) & (token < length)).astype(SINGLE)[None, :, None]
    chosen = (spot_of[:, :, None] == jnp.arange(patches_all)[None, None, :]).astype(HALF)
    patches = jnp.einsum(
        "ctp,cpv->ctv", chosen, pixels, preferred_element_type=SINGLE
    ).astype(HALF)
    row_ids = jnp.arange(spots * sensors * bands)
    row_spot, row_sensor, row_band = (
        row_ids // (sensors * bands),
        (row_ids // bands) % sensors,
        row_ids % bands,
    )
    source = jnp.where(
        row_sensor[None, :] == sensor_id[:, None], (row_band * spots + row_spot)[None, :], -1
    )
    spread = (jnp.arange(pix_width)[None, :, None] == source[:, None, :]).astype(HALF)
    patches_wide = (
        jnp.einsum("ctv,cvr->ctr", patches, spread, preferred_element_type=SINGLE)
        .astype(HALF)
        .reshape(rows_all, -1)
    )
    kern_chip = jnp.einsum(
        "cvr,rd->cvd", spread, generated, preferred_element_type=SINGLE
    ).astype(HALF)

    side_len = jnp.where(chip_size == MAXP, SIDE, SIDE // 2).astype(jnp.int32)[:, None]
    quarter = width // 4
    freqs = 10000.0 ** (-jnp.arange(quarter, dtype=SINGLE) / quarter)
    angles = jnp.arange(SIDE, dtype=SINGLE)[:, None] * freqs
    table = jnp.concatenate([jnp.sin(angles), jnp.cos(angles)], axis=-1)

    def places(steps):
        steps = jnp.where(spot_of < 0, -1, steps)
        hot = (steps[:, :, None] == jnp.arange(SIDE)).astype(SINGLE)
        return jnp.einsum("cts,se->cte", hot, table, precision=PRECISE)

    base = jnp.concatenate(
        [places(spot_of // side_len), places(spot_of % side_len)], axis=-1
    )
    base = base + patch_bias * is_patch
    meta_tok = jnp.dot(time_place, w_meta.astype(SINGLE), precision=PRECISE)
    base = jnp.where((token == 0)[None, :, None], cls_token[None, None, :], base)
    base = jnp.where((token == 1)[None, :, None], meta_tok[:, None, :], base)
    base = base.reshape(rows_all, width)

    counts = (lead + chip_size // 4).astype(jnp.int32)
    keep_rows = (
        (token[None, :] < counts[:, None]).reshape(rows_all, 1).astype(SINGLE)
    )
    grad_final = (
        jnp.pad(cotangent, ((0, 0), (0, rows - length), (0, 0)))
        .reshape(rows_all, width)
        .astype(SINGLE)
        * keep_rows
    )
    grad_branch = grad_final.astype(HALF)
    g_fc2_bias = jnp.sum(grad_final, axis=0)

    start = (
        jnp.dot(patches_wide, generated, preferred_element_type=SINGLE) + base
    )
    normed_one, hat_one, inv_one = norm_forward(start, ln1_gain, ln1_bias)
    normed_one = normed_one.astype(HALF)
    joined = jnp.dot(normed_one, proj_qkv, preferred_element_type=SINGLE).astype(HALF)
    joined = joined.reshape(chips, rows, -1)
    attn = attention_call(
        functools.partial(attend_kernel, width, scale),
        "attend",
        counts,
        (joined,),
        width,
        4 * chips * rows * rows * width,
    ).reshape(rows_all, width)
    middle = start + jnp.dot(attn, proj_out, preferred_element_type=SINGLE) + out_bias
    normed_two, hat_two, inv_two = norm_forward(middle, ln2_gain, ln2_bias)
    normed_two = normed_two.astype(HALF)
    grad_hidden = jnp.einsum(
        "rd,fd->rf", grad_branch, proj_down, preferred_element_type=SINGLE
    )
    pre_up = jnp.dot(normed_two, proj_up, preferred_element_type=SINGLE) + fc1_bias
    hidden_f, hidden_slope = gelu_parts(pre_up)
    hidden = hidden_f.astype(HALF)
    grad_up = (grad_hidden * hidden_slope).astype(HALF)

    g_down = jnp.einsum("rf,rd->fd", hidden, grad_branch, preferred_element_type=SINGLE)
    g_up = jnp.einsum("rd,rf->df", normed_two, grad_up, preferred_element_type=SINGLE)
    g_down, g_up = scatter([g_down.astype(HALF), g_up.astype(HALF)], me, count)
    g_fc1_bias = jnp.sum(grad_up.astype(SINGLE), axis=0)
    grad_norm_two = jnp.einsum(
        "rf,df->rd", grad_up, proj_up, preferred_element_type=SINGLE
    )
    back_two, g_ln2_gain, g_ln2_bias = norm_backward(
        grad_norm_two, hat_two, inv_two, ln2_gain
    )
    grad_middle = grad_final + back_two
    grad_attn_out = grad_middle.astype(HALF)
    g_out_bias = jnp.sum(grad_attn_out.astype(SINGLE), axis=0)
    g_out = jnp.einsum("rd,re->de", attn, grad_attn_out, preferred_element_type=SINGLE)
    grad_attn = (
        jnp.einsum("re,de->rd", grad_attn_out, proj_out, preferred_element_type=SINGLE)
        .astype(HALF)
        .reshape(chips, rows, width)
    )
    grad_joined = attention_call(
        functools.partial(attend_back_kernel, width, scale),
        "attend_back",
        counts,
        (joined, grad_attn),
        3 * width,
        10 * chips * rows * rows * width,
    ).reshape(rows_all, -1)
    g_qkv = jnp.einsum(
        "rd,re->de", normed_one, grad_joined, preferred_element_type=SINGLE
    )
    g_qkv, g_out = scatter([g_qkv.astype(HALF), g_out.astype(HALF)], me, count)
    grad_norm_one = jnp.einsum(
        "re,de->rd", grad_joined, proj_qkv, preferred_element_type=SINGLE
    )
    back_one, g_ln1_gain, g_ln1_bias = norm_backward(
        grad_norm_one, hat_one, inv_one, ln1_gain
    )
    grad_start = grad_middle + back_one
    grad_embedded = (
        (grad_start.reshape(chips, rows, width) * is_patch)
        .astype(HALF)
        .reshape(rows_all, width)
    )
    kern_terms = jnp.einsum(
        "rk,rd->kd", patches_wide, grad_embedded, preferred_element_type=SINGLE
    ).astype(HALF)
    if pieces > 1:
        kern_terms = kern_terms.reshape(
            spots // held, held * sensors * bands, pieces, per_row
        ).transpose(0, 2, 1, 3)
    grad_kernel = scatter([kern_terms.reshape(-1, per_row)], me, count)[0]
    grad_kernel = grad_kernel.reshape(held, sensors * bands, per_row)
    grad_embed = split_dot("prc,pch->rh", grad_kernel, wave2_own)
    g_wave2 = split_dot("prc,rh->pch", grad_kernel, embed_low).reshape(columns, -1)
    by_chip = grad_start.reshape(chips, rows, width)
    g_cls = jnp.sum(by_chip[:, 0, :], axis=0)
    grad_meta = by_chip[:, 1, :]
    g_w_meta = jnp.einsum("cm,cd->md", time_place, grad_meta, precision=PRECISE)
    g_time_place = jnp.einsum(
        "cd,md->cm", grad_meta, w_meta.astype(SINGLE), precision=PRECISE
    )
    g_patch_bias = jnp.sum(by_chip * is_patch, axis=(0, 1))
    meta_rows = time_place.shape[1]
    small = total_over(
        jnp.concatenate(
            [
                g_w_meta,
                g_fc1_bias.reshape(-1, width),
                g_cls[None],
                g_patch_bias[None],
                g_ln1_gain[None],
                g_ln1_bias[None],
                g_out_bias[None],
                g_ln2_gain[None],
                g_ln2_bias[None],
                g_fc2_bias[None],
                jnp.pad(grad_embed.reshape(-1), (0, -grad_embed.size % width)).reshape(
                    -1, width
                ),
            ],
            axis=0,
        ),
        count,
    )
    base_row = meta_rows + fc1_bias.shape[0] // width
    grad_embed = small[base_row + 8 :].reshape(-1)[: grad_embed.size]
    grad_embed = grad_embed.reshape(sensors * bands, -1)
    grad_pre = grad_embed * band_mask * activ_slope
    g_wave1 = jnp.einsum("rh,rk->hk", code, grad_pre, precision=PRECISE)
    g_wave1_bias = jnp.sum(grad_pre, axis=0)


    scattered = jnp.einsum(
        "ctp,ctd->cpd",
        chosen,
        grad_embedded.reshape(chips, rows, width),
        preferred_element_type=SINGLE,
    ).astype(HALF)
    g_pixels = jnp.einsum(
        "cpd,cvd->cpv", scattered, kern_chip, preferred_element_type=SINGLE
    )
    final = middle + jnp.dot(hidden, proj_down, preferred_element_type=SINGLE) + fc2_bias
    mixed = (final * keep_rows).astype(HALF).reshape(chips, rows, width)[:, :length]
    return (
        mixed,
        g_pixels,
        g_time_place,
        small[base_row],
        small[:meta_rows],
        g_wave1,
        g_wave1_bias,
        g_wave2,
        small[base_row + 1],
        small[base_row + 2],
        small[base_row + 3],
        g_qkv,
        g_out,
        small[base_row + 4],
        small[base_row + 5],
        small[base_row + 6],
        g_up,
        small[meta_rows:base_row].reshape(-1),
        g_down,
        small[base_row + 7],
    )


def solution(mesh):
    count = math.prod(mesh.shape[a] for a in AXES)
    split = lambda rank: P(AXES, *([None] * (rank - 1)))
    return jax.shard_map(
        functools.partial(local, count),
        mesh=mesh,
        in_specs=(
            split(3),
            split(2),
            split(1),
            split(1),
            P(),
            P(),
            split(2),
            P(),
            P(),
            P(),
            P(),
            split(2),
            P(),
            P(),
            P(),
            split(2),
            split(2),
            P(),
            P(),
            P(),
            split(2),
            P(),
            split(2),
            P(),
            split(3),
        ),
        out_specs=(
            split(3),
            split(3),
            split(2),
            P(),
            P(),
            P(),
            P(),
            split(2),
            P(),
            P(),
            P(),
            split(2),
            split(2),
            P(),
            P(),
            P(),
            split(2),
            P(),
            split(2),
            P(),
        ),
        check_vma=False,
    )
```

```python
import functools
import math

import jax
import jax.numpy as jnp
from jax import lax
from jax.experimental import pallas as pl
from jax.experimental.pallas import tpu as pltpu
from jax.sharding import PartitionSpec as P

D = 768
HEADS = 12
HYPER = 128
SIDE = 32
MAXP = 1024
AXES = ("sensor", "batch")

PRECISE = lax.Precision.HIGHEST
EPSILON = 1e-05
MASKED = -1e30
SINGLE = jnp.float32
HALF = jnp.bfloat16


def bit_groups(count):
    bits = count.bit_length() - 1
    high = list(range(3, bits))
    groups = [high[i : i + 2] for i in range(0, len(high), 2)]
    groups.append([b for b in (0, 2) if b < bits])
    if bits > 1:
        groups.append([1])
    return groups


def masks_of(group):
    masks = [0]
    for b in group:
        masks = masks + [m ^ (1 << b) for m in masks]
    return masks


def swap(values, mask, count):
    return lax.ppermute(values, AXES, [(i, i ^ mask) for i in range(count)])


def window(ref, first, rows, start, width):
    if rows != ref.shape[-2]:
        ref = ref.at[(slice(None),) * (len(ref.shape) - 2) + (pl.ds(first, rows),)]
    if width != ref.shape[-1]:
        ref = ref.at[(slice(None),) * (len(ref.shape) - 1) + (pl.ds(start, width),)]
    return ref


def place_kernel(offsets, part, splits, index_ref, *refs):
    pieces, refs = refs[: len(offsets)], refs[len(offsets) :]
    outs, (staged, in_sems, out_sems) = refs[:-3], refs[-3:]
    arrive, depart = placing(
        offsets, part, splits, index_ref[0], pieces, outs, staged, in_sems, out_sems
    )
    arrive()
    depart()()


def placing(offsets, part, splits, me, pieces, outs, staged, in_sems, out_sems):
    arrivals, first = [], 0
    for i, piece in enumerate(pieces):
        size = piece.shape[0]
        arrivals.append(
            pltpu.make_async_copy(
                window(piece, *part, 0, piece.shape[-1]),
                staged.at[pl.ds(first, size)],
                in_sems.at[i],
            )
        )
        first += size

    def arrive():
        for arrival in arrivals:
            arrival.start()

    def depart():
        departures, first = [], 0
        for arrival, masks in zip(arrivals, offsets):
            arrival.wait()
            for t, mask in enumerate(masks):
                for which, slot, row, rows, start, width, at in splits:
                    target = outs[which].at[me ^ mask]
                    target = target if slot is None else target.at[slot]
                    source = staged.at[first + t]
                    departures.append(
                        pltpu.make_async_copy(
                            window(source, row, rows, start, width),
                            window(target, 0, rows, at, width),
                            out_sems.at[len(departures)],
                        )
                    )
                    departures[-1].start()
            first += len(masks)

        def wait():
            for departure in departures:
                departure.wait()

        return wait

    return arrive, depart


def place(pieces, masks, part, splits, shapes, index, count):
    kind, width = pieces[0].dtype, pieces[0].shape[-1]
    return pl.pallas_call(
        functools.partial(place_kernel, masks, part, splits),
        out_shape=[jax.ShapeDtypeStruct((count, *s), kind) for s in shapes],
        in_specs=[pl.BlockSpec(memory_space=pltpu.SMEM)]
        + [pl.BlockSpec(memory_space=pl.ANY)] * len(pieces),
        out_specs=[pl.BlockSpec(memory_space=pl.ANY)] * len(shapes),
        scratch_shapes=[
            pltpu.VMEM((count, part[1], width), kind),
            pltpu.SemaphoreType.DMA((len(pieces),)),
            pltpu.SemaphoreType.DMA((count * len(splits),)),
        ],
        compiler_params=pltpu.CompilerParams(vmem_limit_bytes=32 * 2**20),
        cost_estimate=pl.CostEstimate(
            flops=0,
            bytes_accessed=4 * count * part[1] * width,
            transcendentals=0,
        ),
        name="place",
    )(index, *pieces)


def stack_kernel(sizes, *refs):
    total = sum(sizes)
    pieces, outs = refs[:total], refs[total : total + len(sizes)]
    staged, sems = refs[total + len(sizes) : -1], refs[-1]
    arrivals, done = [], 0
    for buffer, size in zip(staged, sizes):
        for i, piece in enumerate(pieces[done : done + size]):
            arrivals.append(
                pltpu.make_async_copy(
                    piece,
                    buffer.at[pl.ds(i * piece.shape[0], piece.shape[0])],
                    sems.at[done + i],
                )
            )
        done += size
    for arrival in arrivals:
        arrival.start()
    departures, done = [], 0
    for o, (buffer, size) in enumerate(zip(staged, sizes)):
        for arrival in arrivals[done : done + size]:
            arrival.wait()
        done += size
        departures.append(
            pltpu.make_async_copy(buffer, outs[o], sems.at[total + o])
        )
        departures[-1].start()
    for departure in departures:
        departure.wait()


def stack(groups):
    pieces = [p for group in groups for p in group]
    kind, tail = pieces[0].dtype, pieces[0].shape[1:]
    shapes = [(sum(p.shape[0] for p in g), *tail) for g in groups]
    return pl.pallas_call(
        functools.partial(stack_kernel, [len(g) for g in groups]),
        out_shape=[jax.ShapeDtypeStruct(s, kind) for s in shapes],
        in_specs=[pl.BlockSpec(memory_space=pl.ANY)] * len(pieces),
        out_specs=[pl.BlockSpec(memory_space=pl.ANY)] * len(groups),
        scratch_shapes=[pltpu.VMEM(s, kind) for s in shapes]
        + [pltpu.SemaphoreType.DMA((len(pieces) + len(groups),))],
        cost_estimate=pl.CostEstimate(
            flops=0,
            bytes_accessed=4 * sum(math.prod(s) for s in shapes),
            transcendentals=0,
        ),
        name="stack",
    )(*pieces)


def join_kernel(parts, *refs):
    arrays, (out, staged, sems) = refs[:-3], refs[-3:]
    copies = []
    for which, row, rows, start, width, to_row, to_start in parts:
        copies.append(
            pltpu.make_async_copy(
                window(arrays[which], row, rows, start, width),
                window(staged, to_row, rows, to_start, width),
                sems.at[len(copies)],
            )
        )
        copies[-1].start()
    for copy in copies:
        copy.wait()
    back = pltpu.make_async_copy(staged, out, sems.at[len(parts)])
    back.start()
    back.wait()


def join(arrays, parts, shape):
    kind = arrays[0].dtype
    return pl.pallas_call(
        functools.partial(join_kernel, parts),
        out_shape=jax.ShapeDtypeStruct(shape, kind),
        in_specs=[pl.BlockSpec(memory_space=pl.ANY)] * len(arrays),
        out_specs=pl.BlockSpec(memory_space=pl.ANY),
        scratch_shapes=[
            pltpu.VMEM(shape, kind),
            pltpu.SemaphoreType.DMA((len(parts) + 1,)),
        ],
        name="join",
    )(*arrays)


class Layout:
    def __init__(self, shards, width):
        rows = min(s.shape[0] for s in shards)
        self.by_rows = width is not None
        self.parts, self.splits, self.shapes, self.shards = [], [], [], shards
        row, column = 0, 0
        for which, shard in enumerate(shards):
            step = width if self.by_rows else shard.shape[1]
            k = 1 if self.by_rows else shard.shape[0] // rows
            size = shard.shape[0] // k
            self.shapes.append((k, size, shard.shape[1]) if k > 1 else shard.shape)
            for i in range(k):
                for start in range(0, shard.shape[1], step):
                    self.parts.append((which, i * size, size, start, step, row, column))
                    self.splits.append(
                        (which, i if k > 1 else None, row, size, column, step, start)
                    )
                    if self.by_rows:
                        row += size
                    else:
                        column += step
        self.shape = (row, width) if self.by_rows else (rows, column)

    def joined(self):
        if len(self.parts) == 1:
            return self.shards[0]
        if not self.by_rows:
            return jnp.concatenate(
                [
                    self.shards[which][row : row + size]
                    for which, row, size, *_ in self.parts
                ],
                axis=1,
            )
        return join(self.shards, self.parts, self.shape)


def after(value, *others):
    return lax.optimization_barrier((value, *others))[0]


Y, CORE, X, Z0 = 1, 2, 4, 8


class Gather:
    def __init__(self, layout, index, count):
        self.layout, self.index, self.count = layout, index, count
        self.data = layout.joined()

    def along_z(self, *others):
        data, masks = after(self.data, *others)[None], [0]
        for b in range(self.count.bit_length() - 2, 3, -1):
            data = stack([[data, swap(data, 1 << b, self.count)]])[0]
            masks = masks + [m ^ (1 << b) for m in masks]
        self.first, self.masks, self.zs = data, masks, [data]
        self.second = swap(data, Z0, self.count)
        return self.second

    def first_xy(self, *others):
        first = after(self.first, *others)
        self.by_y = swap(first, Y, self.count)
        self.by_x = swap(after(self.second, *others), X, self.count)

    def second_xy(self, *others):
        masks = self.masks
        by_y = after(self.by_y, *others)
        (first, second) = stack([[self.first, by_y], [self.second, self.by_x]])
        self.turn = first
        of_first = masks + [m ^ Y for m in masks]
        of_second = [m ^ Z0 for m in masks + [m ^ X for m in masks]]
        self.pieces = [
            (of_first, first),
            (of_second, second),
            ([m ^ X for m in of_first], swap(first, X, self.count)),
            ([m ^ Y for m in of_second], swap(second, Y, self.count)),
        ]
        return [p for _, p in self.pieces[2:]]

    def along_core(self, *others):
        self.pieces = self.pieces + [
            ([m ^ CORE for m in held], swap(after(piece, *others), CORE, self.count))
            for held, piece in self.pieces
        ]

    def finish(self):
        wholes = place(
            [p for _, p in self.pieces],
            [m for m, _ in self.pieces],
            (0, self.layout.shape[0]),
            self.layout.splits,
            self.layout.shapes,
            self.index,
            self.count,
        )
        return [w.reshape(-1, w.shape[-1]) for w in wholes]


def add_kernel(outs_of, index_ref, *refs):
    outs = refs[len(refs) - len(outs_of) :]
    for out, sources in zip(outs, outs_of):
        for first, width, members in sources:
            step = 768 if width % 768 == 0 else width
            for at in range(0, width, step):
                total = None
                for which in members:
                    value = refs[which][0, :, at : at + step].astype(SINGLE)
                    total = value if total is None else total + value
                out[0, :, first + at : first + at + step] = total.astype(out.dtype)


def added(outputs, length, pieces, index, name):
    in_specs, operands, outs_of, out_shape = [], [], [], []
    for (low, high), kind, sources in outputs:
        rows = sources[0][0].shape[1]
        plan = []
        for start, width in pieces:
            if not low <= start < high:
                continue
            members = []
            for array, first, where in sources:
                if not first <= start < first + array.shape[2]:
                    continue
                at = (start - first) // width
                assert at * width == start - first
                in_specs.append(
                    pl.BlockSpec(
                        (1, rows, width),
                        lambda h, ref, where=where, at=at: (where(ref[0], h), 0, at),
                    )
                )
                members.append(len(operands))
                operands.append(array)
            plan.append((start - low, width, members))
        outs_of.append(plan)
        out_shape.append(jax.ShapeDtypeStruct((length, rows, high - low), kind))
    moved = sum(length * math.prod(spec.block_shape) for spec in in_specs)
    return pl.pallas_call(
        functools.partial(add_kernel, outs_of),
        out_shape=out_shape,
        grid_spec=pltpu.PrefetchScalarGridSpec(
            num_scalar_prefetch=1,
            grid=(length,),
            in_specs=in_specs,
            out_specs=[
                pl.BlockSpec((1, *s.shape[1:]), lambda h, ref: (h, 0, 0))
                for s in out_shape
            ],
        ),
        compiler_params=pltpu.CompilerParams(vmem_limit_bytes=32 * 2**20),
        cost_estimate=pl.CostEstimate(
            flops=moved, bytes_accessed=4 * moved, transcendentals=0
        ),
        name=name,
    )(index, *[pltpu.with_memory_space_constraint(a, pltpu.HBM) for a in operands])


def position(mask, count):
    top = count.bit_length() - 2
    high = 0
    for j in range(top - 3):
        high = high | (((mask >> (top - j)) & 1) << j)
    z, x, c, y = (mask >> 3) & 1, (mask >> 2) & 1, (mask >> 1) & 1, mask & 1
    inner, outer = z * x + (1 - z) * y, z * y + (1 - z) * x
    return ((c * 4 + z + 2 * outer) << (top - 2)) + (inner << (top - 3)) + high


class Scatter:
    def __init__(self, count, index, relative=False):
        self.count, self.index, self.relative = count, index, relative
        self.own, self.cores, self.pieces, self.width = [], [], [], 0

    def along_core(self, whole, *others):
        rows, width = whole.shape[0] // self.count, whole.shape[1]
        view = whole.reshape(self.count // 4, 2, 2, rows, width)
        other = 1 - ((self.index[0] >> 1) & 1)
        sending = lax.dynamic_slice_in_dim(view, other, 1, axis=1)
        sending = sending.reshape(self.count // 2, rows, width)
        return self.with_core(whole.reshape(self.count, rows, width), sending, *others)

    def with_core(self, own, sending, *others):
        self.sent = [after(sending, *others)]
        self.own.append((own, self.width))
        self.cores.append((swap(self.sent[0], CORE, self.count), self.width))
        self.pieces.append((self.width, own.shape[2]))
        self.width += own.shape[2]
        return self

    def sources(self, target, extra):
        if self.relative:
            both = lambda me, h: position(target(me, h) ^ me, self.count)
            without = both
        else:
            both = lambda me, h: target(me, h)
            without = lambda me, h: ((target(me, h) >> 2) << 1) | (target(me, h) & 1)
        return (
            [(a, f, both) for a, f in self.own]
            + [(a, f, without) for a, f in self.cores]
            + [(a, 0, lambda me, h, at=at: at(h)) for a, at in extra]
        )

    def sums(self, targets, length, name):
        kind = self.own[0][0].dtype
        return added(
            [((0, self.width), kind, self.sources(t, e)) for t, e in targets],
            length,
            self.pieces,
            self.index,
            name,
        )

    def first_xy(self, *others):
        self.cores = [(after(a, *others), f) for a, f in self.cores]
        to_x, to_y = self.sent = self.sums(
            [
                (lambda me, h: me ^ X ^ (h & 1) ^ ((h >> 1) << 4), []),
                (lambda me, h: me ^ (Y | Z0) ^ ((h & 1) << 2) ^ ((h >> 1) << 4), []),
            ],
            2 * (self.count // 16),
            "add_xy",
        )
        self.by_x, self.by_y = swap(to_x, X, self.count), swap(to_y, Y, self.count)
        return self

    def second_xy(self, *others):
        by_x, by_y = after(self.by_x, *others), self.by_y
        to_y, to_x = self.sent = self.sums(
            [
                (lambda me, h: me ^ Y ^ (h << 4), [(by_x, lambda h: 1 + 2 * h)]),
                (lambda me, h: me ^ (X | Z0) ^ (h << 4), [(by_y, lambda h: 1 + 2 * h)]),
            ],
            self.count // 16,
            "add_yx",
        )
        self.mine = [
            (by_x, lambda h: 2 * h),
            (swap(to_y, Y, self.count), lambda h: h),
        ]
        self.next = [
            (by_y, lambda h: 2 * h),
            (swap(to_x, X, self.count), lambda h: h),
        ]
        return self

    def across_z(self, *others):
        last, where = self.next[1]
        extra = [self.next[0], (after(last, *others), where)]
        self.sent = self.sums(
            [(lambda me, h: me ^ Z0 ^ (h << 4), extra)], self.count // 16, "add_z"
        )
        self.mine.append((swap(self.sent[0], Z0, self.count), lambda h: h))
        return self

    def across_rest(self, *others):
        last, where = self.mine[-1]
        self.mine[-1] = (after(last, *others), where)
        for b in range(self.count.bit_length() - 2, 3, -1):
            far = 1 << (b - 4)
            moved = [(a, lambda h, at=at, far=far: at(h + far)) for a, at in self.mine]
            self.sent = self.sums(
                [(lambda me, h, b=b: me ^ (1 << b) ^ (h << 4), moved)], far, "add_far"
            )
            self.mine.append((swap(self.sent[0], 1 << b, self.count), lambda h: h))
        return self

    def finish(self, *others):
        last, where = self.mine[-1]
        extra = self.mine[:-1] + [(after(last, *others), where)]
        sources = self.sources(lambda me, h: me + h, extra)
        totals = added(
            [((f, f + a.shape[2]), SINGLE, sources) for a, f in self.own],
            1,
            self.pieces,
            self.index,
            "add_last",
        )
        return [t[0] for t in totals]


def pack_rows(arrays, square, width):
    blocks = width // square.shape[1]
    rows = -(-square.shape[0] // (8 * blocks)) * 8
    square = jnp.pad(square, ((0, rows * blocks - square.shape[0]), (0, 0)))
    total = rows + sum(a.size // width for a in arrays)

    def kernel(square_ref, *refs):
        out = refs[-1]
        for i in range(blocks):
            out[:rows, i * 128 : (i + 1) * 128] = square_ref[i * rows : (i + 1) * rows, :]
        first = rows
        for ref in refs[:-1]:
            size = ref.size // width if ref.ndim == 1 else ref.shape[0]
            out[first : first + size, :] = ref[...].reshape(size, width)
            first += size
        if first < out.shape[0]:
            out[first:, :] = jnp.zeros((out.shape[0] - first, width), SINGLE)

    return pl.pallas_call(
        kernel,
        out_shape=jax.ShapeDtypeStruct((-(-total // 8) * 8, width), SINGLE),
        name="pack_rows",
    )(square, *arrays)


def unpack_rows(packed, shapes, square):
    width = packed.shape[1]
    blocks = width // square[1]
    rows = -(-square[0] // (8 * blocks)) * 8
    whole = [packed[:rows, i * square[1] : (i + 1) * square[1]] for i in range(blocks)]
    parts, first = [jnp.concatenate(whole, axis=0)[: square[0]]], rows
    for size, _ in shapes:
        parts.append(packed[first : first + size])
        first += size
    return parts


def tree_sum(values):
    while len(values) > 1:
        values = [values[i] + values[i + 1] for i in range(0, len(values), 2)]
    return values[0]


def total_over(values, count):
    for group in reversed(bit_groups(count)):
        values = tree_sum(
            [values if m == 0 else swap(values, m, count) for m in masks_of(group)]
        )
    return values


def scores_of(keyed, query, lanes, key_ok):
    own = jnp.where(lanes, keyed, jnp.zeros_like(keyed))
    scores = lax.dot_general(
        own, query, (((1,), (1,)), ((), ())), preferred_element_type=SINGLE
    )
    scores = jnp.where(key_ok, scores, MASKED)
    expd = jnp.exp(scores - jnp.max(scores, axis=0))
    return expd / jnp.sum(expd, axis=0)


def over_rows(left, right):
    return lax.dot_general(
        left, right, (((0,), (0,)), ((), ())), preferred_element_type=SINGLE
    )


def attend_kernel(width, scale, count_ref, qkv_ref, out_ref):
    rows = qkv_ref.shape[1]
    head_dim = width // HEADS
    limit = count_ref[pl.program_id(0)]
    lane = lax.broadcasted_iota(jnp.int32, (rows, 128), 1) // head_dim
    key_ok = lax.broadcasted_iota(jnp.int32, (rows, rows), 0) < limit

    @pl.loop(0, width // 128)
    def _(pair):
        start = pl.multiple_of(pair * 128, 128)
        query = qkv_ref[0, :, pl.ds(start, 128)] * jnp.asarray(scale, HALF)
        keyed = qkv_ref[0, :, pl.ds(pl.multiple_of(width + start, 128), 128)]
        valued = qkv_ref[0, :, pl.ds(pl.multiple_of(2 * width + start, 128), 128)]
        result = jnp.zeros((rows, 128), SINGLE)
        for head in range(128 // head_dim):
            probs = scores_of(keyed, query, lane == head, key_ok)
            result = jnp.where(
                lane == head, over_rows(probs.astype(HALF), valued), result
            )
        out_ref[0, :, pl.ds(start, 128)] = result.astype(HALF)


def attend_back_kernel(width, scale, count_ref, qkv_ref, up_ref, out_ref):
    rows = qkv_ref.shape[1]
    head_dim = width // HEADS
    limit = count_ref[pl.program_id(0)]
    lane = lax.broadcasted_iota(jnp.int32, (rows, 128), 1) // head_dim
    key_ok = lax.broadcasted_iota(jnp.int32, (rows, rows), 0) < limit

    @pl.loop(0, width // 128)
    def _(pair):
        start = pl.multiple_of(pair * 128, 128)
        at_key = pl.multiple_of(width + start, 128)
        at_value = pl.multiple_of(2 * width + start, 128)
        query = qkv_ref[0, :, pl.ds(start, 128)] * jnp.asarray(scale, HALF)
        keyed = qkv_ref[0, :, pl.ds(at_key, 128)]
        valued = qkv_ref[0, :, pl.ds(at_value, 128)]
        upstream = up_ref[0, :, pl.ds(start, 128)]
        grad_q = jnp.zeros((rows, 128), SINGLE)
        grad_k = jnp.zeros((rows, 128), SINGLE)
        grad_v = jnp.zeros((rows, 128), SINGLE)
        for head in range(128 // head_dim):
            own = lane == head
            probs = scores_of(keyed, query, own, key_ok)
            grad_v = jnp.where(
                own,
                jnp.dot(probs.astype(HALF), upstream, preferred_element_type=SINGLE),
                grad_v,
            )
            grad_prob = lax.dot_general(
                jnp.where(own, valued, jnp.zeros_like(valued)),
                upstream,
                (((1,), (1,)), ((), ())),
                preferred_element_type=SINGLE,
            )
            inner = jnp.sum(probs * grad_prob, axis=0)
            grad_score = (probs * (grad_prob - inner)).astype(HALF)
            grad_k = jnp.where(
                own, jnp.dot(grad_score, query, preferred_element_type=SINGLE), grad_k
            )
            grad_q = jnp.where(own, over_rows(grad_score, keyed), grad_q)
        out_ref[0, :, pl.ds(start, 128)] = (grad_q * scale).astype(HALF)
        out_ref[0, :, pl.ds(at_key, 128)] = grad_k.astype(HALF)
        out_ref[0, :, pl.ds(at_value, 128)] = grad_v.astype(HALF)


def embed_kernel(chips, wide_ref, base_ref, gain_ref, offset_ref, *refs):
    pieces, (start_ref, hat_ref, inv_ref, out_ref, whole_ref, staged, sems) = refs[:-7], refs[-7:]
    copies, first = [], 0
    for i, piece in enumerate(pieces):
        size = piece.shape[0]
        copies.append(
            pltpu.make_async_copy(piece, staged.at[pl.ds(first, size)], sems.at[i])
        )
        first += size
    for copy in copies:
        copy.start()
    for copy in copies:
        copy.wait()
    back = pltpu.make_async_copy(staged, whole_ref, sems.at[len(copies)])
    back.start()
    rows = wide_ref.shape[0] // chips

    @pl.loop(0, chips)
    def _(c):
        at = pl.ds(pl.multiple_of(c * rows, rows), rows)
        start = base_ref[at, :] + jnp.dot(
            wide_ref[at, :], staged[...], preferred_element_type=SINGLE
        )
        result, normed, inv_std = norm_forward(start, gain_ref[...], offset_ref[...])
        start_ref[at, :] = start
        hat_ref[at, :] = normed
        inv_ref[at, :] = inv_std
        out_ref[at, :] = result.astype(HALF)

    back.wait()


def embed(chips, wide, base, gain, offset, pieces):
    rows, width = base.shape
    whole = pl.BlockSpec(memory_space=pltpu.VMEM)
    return pl.pallas_call(
        functools.partial(embed_kernel, chips),
        out_shape=[
            jax.ShapeDtypeStruct((rows, width), SINGLE),
            jax.ShapeDtypeStruct((rows, width), SINGLE),
            jax.ShapeDtypeStruct((rows, 1), SINGLE),
            jax.ShapeDtypeStruct((rows, width), HALF),
            jax.ShapeDtypeStruct((wide.shape[1], width), HALF),
        ],
        in_specs=[whole] * 4 + [pl.BlockSpec(memory_space=pl.ANY)] * len(pieces),
        out_specs=[whole] * 4 + [pl.BlockSpec(memory_space=pl.ANY)],
        scratch_shapes=[
            pltpu.VMEM((wide.shape[1], width), HALF),
            pltpu.SemaphoreType.DMA((len(pieces) + 1,)),
        ],
        compiler_params=pltpu.CompilerParams(vmem_limit_bytes=40 * 2**20),
        cost_estimate=pl.CostEstimate(
            flops=2 * rows * wide.shape[1] * width,
            bytes_accessed=2 * wide.size + 2 * wide.shape[1] * width + 14 * base.size,
            transcendentals=0,
        ),
        name="embed",
    )(wide, base, gain[None], offset[None], *pieces)


def attention_call(kernel, name, counts, arrays, out_width, flops):
    chips, rows = arrays[0].shape[:2]

    def spec(columns):
        return pl.BlockSpec((1, rows, columns), lambda c, counts: (c, 0, 0))

    return pl.pallas_call(
        kernel,
        out_shape=jax.ShapeDtypeStruct((chips, rows, out_width), HALF),
        grid_spec=pltpu.PrefetchScalarGridSpec(
            num_scalar_prefetch=1,
            grid=(chips,),
            in_specs=[spec(a.shape[2]) for a in arrays],
            out_specs=spec(out_width),
        ),
        compiler_params=pltpu.CompilerParams(vmem_limit_bytes=40 * 2**20),
        cost_estimate=pl.CostEstimate(
            flops=flops, bytes_accessed=10 * 2**20, transcendentals=2 * 2**20
        ),
        name=name,
    )(counts, *arrays)


def wave_code(wavelengths):
    halfwidth = HYPER // 2
    freqs = 10000.0 ** (-jnp.arange(halfwidth, dtype=SINGLE) / halfwidth)
    angles = (wavelengths * 1000.0)[:, :, None] * freqs
    return jnp.concatenate([jnp.sin(angles), jnp.cos(angles)], axis=-1)


def norm_forward(values, gain, offset):
    center = values - jnp.mean(values, axis=-1, keepdims=True)
    inv_std = lax.rsqrt(jnp.mean(center * center, axis=-1, keepdims=True) + EPSILON)
    normed = center * inv_std
    return (normed * gain + offset, normed, inv_std)


def norm_backward(upstream, normed, inv_std, gain):
    scaled = upstream * gain
    back = inv_std * (
        scaled
        - jnp.mean(scaled, axis=-1, keepdims=True)
        - normed * jnp.mean(scaled * normed, axis=-1, keepdims=True)
    )
    return (
        back,
        jnp.sum(upstream * normed, axis=0),
        jnp.sum(upstream, axis=0),
    )


def gelu_parts(values):
    cumul = 0.5 * (1.0 + lax.erf(values * 0.5**0.5))
    density = jnp.exp(-0.5 * values * values) * (2.0 * math.pi) ** (-0.5)
    return (values * cumul, cumul + values * density)


def split_dot(form, exact, other):
    upper = exact.astype(HALF)
    lower = (exact - upper.astype(SINGLE)).astype(HALF)
    first_term = jnp.einsum(form, upper, other, preferred_element_type=SINGLE)
    return first_term + jnp.einsum(form, lower, other, preferred_element_type=SINGLE)


def local(
    count,
    pixels,
    visible,
    chip_size,
    sensor_id,
    band_count,
    wavelengths,
    time_place,
    cls_token,
    w_meta,
    w_wave1,
    wave1_bias,
    w_wave2,
    patch_bias,
    ln1_gain,
    ln1_bias,
    w_qkv,
    w_out,
    out_bias,
    ln2_gain,
    ln2_bias,
    w_fc1,
    fc1_bias,
    w_fc2,
    fc2_bias,
    cotangent,
):
    chips, patches_all, pix_width = pixels.shape
    sensors, bands = wavelengths.shape
    length, width = cotangent.shape[1:]
    seen = visible.shape[1]
    lead = length - seen
    rows = -(-length // 16) * 16
    rows_all = chips * rows
    spots = pix_width // bands
    scale = (width // HEADS) ** (-0.5)
    me = lax.axis_index(AXES).astype(jnp.int32).reshape(1)

    feed_layout = Layout([w_fc1, w_fc2], None)
    feed = lax.all_gather(feed_layout.joined(), AXES, axis=0, tiled=False)

    code = wave_code(wavelengths).reshape(sensors * bands, -1)
    band_mask = (
        (jnp.arange(bands)[None, :] < band_count[:, None]).astype(SINGLE).reshape(-1, 1)
    )
    pre_act = jnp.dot(code, w_wave1.astype(SINGLE), precision=PRECISE) + wave1_bias
    activ, activ_slope = gelu_parts(pre_act)
    embed_low = (activ * band_mask).astype(HALF)
    columns = w_wave2.shape[0]
    held = max(1, columns // width)
    per_row = columns // held
    pieces = width // per_row
    wave2_own = w_wave2.reshape(held, per_row, -1)
    kernel_own = (
        jnp.einsum("rh,pch->prc", embed_low, wave2_own, preferred_element_type=SINGLE)
        .astype(HALF)
        .reshape(held * sensors * bands, per_row)
    )
    merged = pieces == 1 and w_qkv.shape[0] % 8 == 0
    gather_kernel = Gather(Layout([kernel_own], None), me, count)
    z_kernel = gather_kernel.along_z()
    gather_attn = Gather(Layout([w_qkv, w_out], None), me, count)
    gather_attn.data = after(gather_attn.data, gather_kernel.first)

    spot_of = jnp.pad(visible, ((0, 0), (lead, rows - length)), constant_values=-1)
    token = jnp.arange(rows)
    is_patch = ((token >= lead) & (token < length)).astype(SINGLE)[None, :, None]
    chosen = (spot_of[:, :, None] == jnp.arange(patches_all)[None, None, :]).astype(HALF)
    patches = jnp.einsum(
        "ctp,cpv->ctv", chosen, pixels, preferred_element_type=SINGLE
    ).astype(HALF)
    row_ids = jnp.arange(spots * sensors * bands)
    row_spot, row_sensor, row_band = (
        row_ids // (sensors * bands),
        (row_ids // bands) % sensors,
        row_ids % bands,
    )
    if merged:
        order = sorted(range(count), key=lambda mask: position(mask, count))
        block = jnp.asarray(order, jnp.int32)[row_spot // held]
        row_spot = (block ^ me[0]) * held + row_spot % held
    source = jnp.where(
        row_sensor[None, :] == sensor_id[:, None], (row_band * spots + row_spot)[None, :], -1
    )
    spread = (jnp.arange(pix_width)[None, :, None] == source[:, None, :]).astype(HALF)
    patches_wide = (
        jnp.einsum("ctv,cvr->ctr", patches, spread, preferred_element_type=SINGLE)
        .astype(HALF)
        .reshape(rows_all, -1)
    )
    gather_kernel.first_xy(patches_wide)
    gather_attn.along_z()
    gather_kernel.second_xy(*gather_attn.zs)
    gather_attn.first_xy(gather_kernel.turn)
    side_len = jnp.where(chip_size == MAXP, SIDE, SIDE // 2).astype(jnp.int32)[:, None]
    quarter = width // 4
    freqs = 10000.0 ** (-jnp.arange(quarter, dtype=SINGLE) / quarter)
    angles = jnp.arange(SIDE, dtype=SINGLE)[:, None] * freqs
    table = jnp.concatenate([jnp.sin(angles), jnp.cos(angles)], axis=-1)

    def places(steps):
        steps = jnp.where(spot_of < 0, -1, steps)
        hot = (steps[:, :, None] == jnp.arange(SIDE)).astype(SINGLE)
        return jnp.einsum("cts,se->cte", hot, table, precision=PRECISE)

    base = jnp.concatenate(
        [places(spot_of // side_len), places(spot_of % side_len)], axis=-1
    )
    base = base + patch_bias * is_patch
    meta_tok = jnp.dot(time_place, w_meta.astype(SINGLE), precision=PRECISE)
    base = jnp.where((token == 0)[None, :, None], cls_token[None, None, :], base)
    base = jnp.where((token == 1)[None, :, None], meta_tok[:, None, :], base)
    base = base.reshape(rows_all, width)

    counts = (lead + chip_size // 4).astype(jnp.int32)
    keep_rows = (
        (token[None, :] < counts[:, None]).reshape(rows_all, 1).astype(SINGLE)
    )
    grad_final = (
        jnp.pad(cotangent, ((0, 0), (0, rows - length), (0, 0)))
        .reshape(rows_all, width)
        .astype(SINGLE)
        * keep_rows
    )
    grad_branch = grad_final.astype(HALF)
    g_fc2_bias = jnp.sum(grad_final, axis=0)

    gather_kernel.along_core(base, grad_branch)
    own_pieces = [p for _, p in gather_kernel.pieces]
    gather_attn.second_xy(*own_pieces[2:4])
    if merged:
        assert [m for ms, _ in gather_kernel.pieces for m in ms] == order
        start, hat_one, inv_one, normed_one, generated = embed(
            chips,
            patches_wide,
            after(base, gather_attn.turn),
            ln1_gain,
            ln1_bias,
            [p.reshape(-1, width) for p in own_pieces],
        )
    else:
        generated = gather_kernel.finish()[0].reshape(
            spots // held, pieces, held * sensors * bands, per_row
        )
        generated = generated.transpose(0, 2, 1, 3).reshape(-1, width)
        start = base + jnp.dot(patches_wide, generated, preferred_element_type=SINGLE)
        normed_one, hat_one, inv_one = norm_forward(start, ln1_gain, ln1_bias)
        normed_one = normed_one.astype(HALF)
    proj_up, proj_down = place(
        [after(feed, start)],
        [list(range(count))],
        (0, feed_layout.shape[0]),
        feed_layout.splits,
        feed_layout.shapes,
        jnp.zeros_like(me),
        count,
    )
    proj_up, proj_down = proj_up.reshape(width, -1), proj_down.reshape(-1, width)
    gather_attn.along_core(proj_up)
    proj_qkv, proj_out = gather_attn.finish()
    joined = jnp.dot(normed_one, proj_qkv, preferred_element_type=SINGLE).astype(HALF)
    joined = joined.reshape(chips, rows, -1)
    attn = attention_call(
        functools.partial(attend_kernel, width, scale),
        "attend",
        counts,
        (joined,),
        width,
        4 * chips * rows * rows * width,
    ).reshape(rows_all, width)
    middle = start + jnp.dot(attn, proj_out, preferred_element_type=SINGLE) + out_bias
    normed_two, hat_two, inv_two = norm_forward(middle, ln2_gain, ln2_bias)
    normed_two = normed_two.astype(HALF)
    grad_hidden = jnp.einsum(
        "rd,fd->rf", grad_branch, proj_down, preferred_element_type=SINGLE
    )
    pre_up = jnp.dot(normed_two, proj_up, preferred_element_type=SINGLE) + fc1_bias
    hidden_f, hidden_slope = gelu_parts(pre_up)
    hidden = hidden_f.astype(HALF)
    grad_up = (grad_hidden * hidden_slope).astype(HALF)

    g_down = jnp.einsum(
        "rf,rd->fd", hidden, grad_branch, preferred_element_type=SINGLE
    ).astype(HALF)
    g_up = jnp.einsum(
        "rd,rf->df", normed_two, grad_up, preferred_element_type=SINGLE
    ).astype(HALF)
    grad_up, g_up, g_down = lax.optimization_barrier((grad_up, g_up, g_down))
    scatter_up = Scatter(count, me).along_core(g_up)
    g_down = lax.psum_scatter(g_down, AXES, scatter_dimension=0, tiled=True)
    grad_up = after(grad_up, *scatter_up.sent)
    g_fc1_bias = jnp.sum(grad_up.astype(SINGLE), axis=0)
    grad_norm_two = jnp.einsum(
        "rf,df->rd", grad_up, proj_up, preferred_element_type=SINGLE
    )
    back_two, g_ln2_gain, g_ln2_bias = norm_backward(
        grad_norm_two, hat_two, inv_two, ln2_gain
    )
    grad_middle = grad_final + back_two
    grad_attn_out = grad_middle.astype(HALF)
    g_out_bias = jnp.sum(grad_attn_out.astype(SINGLE), axis=0)
    g_out = jnp.einsum(
        "rd,re->de", attn, grad_attn_out, preferred_element_type=SINGLE
    ).astype(HALF)
    grad_attn = (
        jnp.einsum("re,de->rd", grad_attn_out, proj_out, preferred_element_type=SINGLE)
        .astype(HALF)
        .reshape(chips, rows, width)
    )
    scatter_up.first_xy(grad_attn)
    grad_attn = after(grad_attn, *scatter_up.sent)
    grad_joined = attention_call(
        functools.partial(attend_back_kernel, width, scale),
        "attend_back",
        counts,
        (joined, grad_attn),
        3 * width,
        10 * chips * rows * rows * width,
    ).reshape(rows_all, -1)
    scatter_up.second_xy(grad_joined)
    g_qkv = jnp.einsum(
        "rd,re->de",
        normed_one,
        after(grad_joined, *scatter_up.sent),
        preferred_element_type=SINGLE,
    ).astype(HALF)
    scatter_attn = Scatter(count, me).along_core(g_qkv)
    grad_norm_one = jnp.einsum(
        "re,de->rd",
        after(grad_joined, *scatter_attn.sent),
        proj_qkv,
        preferred_element_type=SINGLE,
    )
    scatter_attn.along_core(g_out)
    back_one, g_ln1_gain, g_ln1_bias = norm_backward(
        grad_norm_one, hat_one, inv_one, ln1_gain
    )
    grad_start = grad_middle + back_one
    grad_embedded = (
        (grad_start.reshape(chips, rows, width) * is_patch)
        .astype(HALF)
        .reshape(rows_all, width)
    )
    scatter_up.across_z(grad_embedded)
    scatter_attn.first_xy(grad_embedded)
    grad_late = after(grad_embedded, *scatter_up.sent, *scatter_attn.sent)
    scatter_kernel = Scatter(count, me, relative=merged)

    def kernel_terms(wide):
        return jnp.einsum(
            "rk,rd->kd", wide, grad_late, preferred_element_type=SINGLE
        ).astype(HALF)

    if merged:
        half = patches_wide.shape[1] // 2
        far = kernel_terms(patches_wide[:, half:]).reshape(count // 2, -1, width)
        kern_terms = kernel_terms(after(patches_wide, far)[:, :half])
        scatter_kernel.with_core(kern_terms.reshape(count // 2, -1, width), far)
    else:
        kern_terms = kernel_terms(patches_wide)
        if pieces > 1:
            kern_terms = kern_terms.reshape(
                spots // held, held * sensors * bands, pieces, per_row
            ).transpose(0, 2, 1, 3)
        scatter_kernel.along_core(kern_terms.reshape(-1, per_row))
    scatter_up.across_rest(kern_terms)
    scatter_kernel.first_xy(*scatter_up.sent)
    kern_chip = jnp.einsum(
        "cvr,rd->cvd",
        spread,
        after(generated, *scatter_kernel.sent),
        preferred_element_type=SINGLE,
    ).astype(HALF)
    scatter_attn.second_xy(kern_chip)
    scatter_kernel.second_xy(*scatter_attn.sent)
    final = middle + jnp.dot(
        after(hidden, *scatter_kernel.sent), proj_down, preferred_element_type=SINGLE
    )
    mixed = ((final + fc2_bias) * keep_rows).astype(HALF)
    mixed = mixed.reshape(chips, rows, width)[:, :length]
    scatter_attn.across_z(mixed)
    scatter_kernel.across_z(*scatter_attn.sent)
    scattered = jnp.einsum(
        "ctp,ctd->cpd",
        chosen,
        after(grad_embedded, *scatter_kernel.sent).reshape(chips, rows, width),
        preferred_element_type=SINGLE,
    ).astype(HALF)
    scatter_kernel.across_rest(scattered)
    scatter_attn.across_rest(*scatter_kernel.sent)
    g_pixels = jnp.einsum(
        "cpd,cvd->cpv",
        after(scattered, *scatter_attn.sent),
        kern_chip,
        preferred_element_type=SINGLE,
    )
    grad_kernel = scatter_kernel.finish(g_pixels)[0]
    grad_kernel = grad_kernel.reshape(held, sensors * bands, per_row)
    grad_embed = split_dot("prc,pch->rh", grad_kernel, wave2_own)
    g_wave2 = split_dot("prc,rh->pch", grad_kernel, embed_low).reshape(columns, -1)
    by_chip = grad_start.reshape(chips, rows, width)
    g_cls = jnp.sum(by_chip[:, 0, :], axis=0)
    grad_meta = by_chip[:, 1, :]
    g_w_meta = jnp.einsum("cm,cd->md", time_place, grad_meta, precision=PRECISE)
    g_time_place = jnp.einsum(
        "cd,md->cm", grad_meta, w_meta.astype(SINGLE), precision=PRECISE
    )
    g_patch_bias = jnp.sum(
        (by_chip * is_patch).reshape(rows_all, width), axis=0, keepdims=True
    )
    ups = fc1_bias.shape[0] // width
    shapes = [(time_place.shape[1], width), (ups, width)] + [(1, width)] * 8
    packed = pack_rows(
        [
            g_w_meta,
            *[g_fc1_bias[i * width : (i + 1) * width] for i in range(ups)],
            g_cls,
            g_patch_bias,
            g_ln1_gain,
            g_ln1_bias,
            g_out_bias,
            g_ln2_gain,
            g_ln2_bias,
            g_fc2_bias,
        ],
        grad_embed,
        width,
    )
    g_down = after(g_down, packed).astype(SINGLE)
    g_up = scatter_up.finish(packed)[0]
    g_qkv, g_out = scatter_attn.finish(packed)
    packed = total_over(packed, count)
    grad_embed, *small = unpack_rows(packed, shapes, grad_embed.shape)
    grad_pre = grad_embed * band_mask * activ_slope
    g_wave1 = jnp.einsum("rh,rk->hk", code, grad_pre, precision=PRECISE)
    g_wave1_bias = jnp.sum(grad_pre, axis=0)
    return (
        mixed,
        g_pixels,
        g_time_place,
        small[2].reshape(-1),
        small[0],
        g_wave1,
        g_wave1_bias,
        g_wave2,
        small[3].reshape(-1),
        small[4].reshape(-1),
        small[5].reshape(-1),
        g_qkv,
        g_out,
        small[6].reshape(-1),
        small[7].reshape(-1),
        small[8].reshape(-1),
        g_up,
        small[1].reshape(-1),
        g_down,
        small[9].reshape(-1),
    )


def solution(mesh):
    count = math.prod(mesh.shape[a] for a in AXES)
    split = lambda rank: P(AXES, *([None] * (rank - 1)))
    return jax.shard_map(
        functools.partial(local, count),
        mesh=mesh,
        in_specs=(
            split(3),
            split(2),
            split(1),
            split(1),
            P(),
            P(),
            split(2),
            P(),
            P(),
            P(),
            P(),
            split(2),
            P(),
            P(),
            P(),
            split(2),
            split(2),
            P(),
            P(),
            P(),
            split(2),
            P(),
            split(2),
            P(),
            split(3),
        ),
        out_specs=(
            split(3),
            split(3),
            split(2),
            P(),
            P(),
            P(),
            P(),
            split(2),
            P(),
            P(),
            P(),
            split(2),
            split(2),
            P(),
            P(),
            P(),
            split(2),
            P(),
            split(2),
            P(),
        ),
        check_vma=False,
    )
```
